1024 devices in a mesh: energy: 128 (over x, z_hi, y, core), slab: 8 (over z_lo).
Axes of the slice: x: 4, y: 8, z: 16 (z_hi: 2, z_lo: 8; z = z_hi * 8 + z_lo), core: 2. Of those that a mesh axis runs over, the one named last changes fastest.
Arguments:
- green: bfloat16 [128, 8, 2, 384, 384], P('energy', 'slab'), may hold values from -6 to 6
- weights: int32 [128, 2, 2], P('energy'), may hold values from 1 to 63
- coupling_m: bfloat16 [2, 384, 384], replicated, may hold values from -0.3125 to 0.3125
- coupling_n: bfloat16 [2, 384, 384], replicated, may hold values from -0.3125 to 0.3125
Outputs:
- sigma: bfloat16 [128, 8, 2, 384, 384], P('energy', 'slab')
The draws below stay inside these ranges and needn't reach their ends.
All inputs are finite; a program needn't handle non-finite values.
Results may differ from the reference program's by a relative error of at most 0.0061.
Values may be sent and summed in bfloat16 or wider, within the bound.
A program may use at most 32 MiB of HBM per device.

```python
import jax
import jax.numpy as jnp
from jax import lax

B = 384
MODES = 2
K1 = 3
K2 = 7
NE = 128
NS = 8


def touch_ends(array, stream_key, smallest, largest):
    dims = array.shape
    spot = [jax.random.randint(jax.random.fold_in(stream_key, axis), (), 0, dims[axis]) for axis in range(len(dims))]
    array = array.at[tuple(spot)].set(smallest)
    longest = dims.index(max(dims))
    spot[longest] = (spot[longest] + 1) % dims[longest]
    return array.at[tuple(spot)].set(largest)


def levels(own_key, extent, split, least, high):
    def one(position, blocks):
        draws = jax.random.uniform(jax.random.fold_in(jax.random.fold_in(own_key, 6), position), (blocks,), jnp.float32, least / len(split), high / len(split))
        return jnp.repeat(jnp.exp(draws), extent[position] // blocks).reshape((-1,) + (1,) * (len(extent) - position - 1))

    gain = one(*split[0])
    for cut in split[1:]:
        gain = gain * one(*cut)
    return gain


def gaussian(key, shape, spread, limit, pieces=(), kind=jnp.bfloat16):
    level = levels(key, shape, pieces, -0.22, 0.18) if pieces else 1.0
    values = jax.random.normal(key, shape, jnp.float32) * spread * level
    return jnp.minimum(jnp.maximum(values, -limit), limit).astype(kind)


def setup_inputs(seed: int = 0) -> dict:
    key_list = jax.random.split(jax.random.key(seed), 5)
    return {
        "green": gaussian(key_list[0], (NE, NS, 2, B, B), 1.0, 6.0, ((0, 128), (1, 8))),
        "weights": touch_ends(jax.random.randint(key_list[1], (NE, MODES, 2), 1, 64), jax.random.fold_in(key_list[1], 1), 1, 63).astype(jnp.int32),
        "coupling_m": gaussian(key_list[2], (MODES, B, B), B ** -0.5, 0.3125),
        "coupling_n": gaussian(key_list[3], (MODES, B, B), B ** -0.5, 0.3125),
    }


def transform(mat, combo):
    left = jnp.einsum('ij,spjk->spik', mat.astype(jnp.float32), combo.astype(jnp.float32)).astype(jnp.bfloat16)
    return left, mat


def apply_right(left, mat):
    return jnp.einsum('spik,lk->spil', left.astype(jnp.float32), mat.astype(jnp.float32))


def reference(green, weights, coupling_m, coupling_n):
    shifts = (K1, K2)
    count = green.shape[0]

    def one_energy(index):
        own = jnp.zeros(green.shape[1:], jnp.float32)
        term = jnp.zeros(green.shape[1:], jnp.float32)
        for mode in range(MODES):
            step = shifts[mode]
            up_index = index + step
            down_index = index - step
            up_valid = (up_index < count).astype(jnp.float32)
            down_valid = (down_index >= 0).astype(jnp.float32)
            upper = lax.dynamic_index_in_dim(green, jnp.clip(up_index, 0, count - 1).astype(jnp.int32), 0, False).astype(jnp.float32)
            lower = lax.dynamic_index_in_dim(green, jnp.clip(down_index, 0, count - 1).astype(jnp.int32), 0, False).astype(jnp.float32)
            wrow = lax.dynamic_index_in_dim(weights, index.astype(jnp.int32), 0, False).astype(jnp.float32) / 32.0
            combo = (wrow[mode, 0] * up_valid * upper + wrow[mode, 1] * down_valid * lower).astype(jnp.bfloat16)
            left_m, mat_m = transform(coupling_m[mode], combo)
            left_n, mat_n = transform(coupling_n[mode], combo)
            own = own + apply_right(left_m, mat_m)
            term = term + apply_right(left_n, mat_n)
        term = term.astype(jnp.bfloat16).astype(jnp.float32)
        shifted = jnp.concatenate([term[1:], jnp.zeros_like(term[:1])], axis=0)
        return (own + shifted).astype(jnp.bfloat16)

    return lax.map(one_energy, jnp.arange(count, dtype=jnp.int32))
```

```python
import functools

import jax
import jax.numpy as jnp
from jax import lax
from jax.experimental import pallas as pl
from jax.experimental.pallas import tpu as pltpu
from jax.sharding import PartitionSpec as P

MESH = pl.DeviceIdType.MESH
RUN = 16
ROWS = 128
A, B, C, D, IMG = range(5)
F32, BF16 = jnp.float32, jnp.bfloat16


def kernel(
    energies,
    slabs,
    green,
    weights,
    coup_m,
    coup_n,
    out,
    held,
    own,
    term,
    term_out,
    term_in,
    right,
    left_m,
    left_n,
    send_sem,
    recv_sem,
    term_send,
    term_recv,
):
    e, s = lax.axis_index("energy"), lax.axis_index("slab")
    size = green.shape[-1]
    per_part = size // ROWS
    chunks = 2 * per_part
    run, p = lax.div(e, RUN), lax.rem(e, RUN)
    first, last = run == 0, run == energies // RUN - 1

    def at(shift):
        return (run * RUN + lax.rem(p + shift + RUN, RUN), s)

    def both(*conds):
        return functools.reduce(jnp.logical_and, conds)

    def either(a, b):
        return jnp.logical_or(a, b)

    inner_up, inner_down = p >= 9, p <= 6
    has_up = both(inner_up, jnp.logical_not(first))
    has_down = both(inner_down, jnp.logical_not(last))
    has_image = either(has_up, has_down)
    got = {A: e >= 3, B: e >= 7, C: e < energies - 3, D: e < energies - 7}

    up_own, down_own = p + 3 < RUN, p >= 3
    sends = {
        "near_up": (either(up_own, has_up), at(3), A),
        "near_down": (either(down_own, has_down), at(-3), C),
        "relay_up": (both(p + 4 < RUN, got[A]), at(4), B),
        "relay_down": (both(p >= 4, got[C]), at(-4), D),
        "far_up": (both(has_up, p <= 12), at(7), B),
        "far_down": (both(has_down, p >= 3), at(-7), D),
        "image_up": (both(inner_up, jnp.logical_not(last)), (e + RUN, s), IMG),
        "image_down": (both(inner_down, jnp.logical_not(first)), (e - RUN, s), IMG),
    }
    number = {name: i for i, name in enumerate(sends)}
    term_goes, term_comes = s > 0, s < slabs - 1

    sources = [
        (got[A], at(-3)),
        (got[C], at(3)),
        (both(got[B], p >= 4), at(-4)),
        (both(got[B], p < 4), at(-7)),
        (both(got[D], p + 4 < RUN), at(4)),
        (both(got[D], p + 4 >= RUN), at(7)),
        (has_up, (e - RUN, s)),
        (has_down, (e + RUN, s)),
        (term_comes, (e, s + 1)),
    ]
    barrier = pltpu.get_barrier_semaphore()
    for cond, where in sources:

        @pl.when(cond)
        def _():
            pl.semaphore_signal(barrier, inc=1, device_id=where, device_id_type=MESH)

    count = sum(cond.astype(jnp.int32) for cond, _, _ in sends.values())
    pl.semaphore_wait(barrier, count + term_goes.astype(jnp.int32))

    def piece(ref, c):
        return ref.at[lax.div(c, per_part), pl.ds(lax.rem(c, per_part) * ROWS, ROWS)]

    def copy(name, source, c):
        _, where, slot = sends[name]
        i = number[name]
        return pltpu.make_async_remote_copy(
            piece(source, c),
            piece(held.at[slot], c),
            send_sem.at[i, c],
            recv_sem.at[slot, c],
            device_id=where,
            device_id_type=MESH,
        )

    def arrived(slot, c):
        pltpu.make_async_remote_copy(
            piece(held.at[slot], c),
            piece(held.at[slot], c),
            send_sem.at[0, c],
            recv_sem.at[slot, c],
            device_id=at(3),
            device_id_type=MESH,
        ).wait_recv()

    mine = green.at[0, 0]

    def start(name, cond, source, c):
        @pl.when(cond)
        def _():
            copy(name, source, c).start()

    @pl.loop(0, chunks)
    def _(c):
        start("image_up", sends["image_up"][0], mine, c)
        start("image_down", sends["image_down"][0], mine, c)
        start("near_up", up_own, mine, c)
        start("near_down", down_own, mine, c)

    for slot, there in got.items():

        @pl.when(jnp.logical_not(there))
        def _():
            held[slot] = jnp.zeros(held.shape[1:], BF16)

    @pl.when(jnp.logical_not(term_comes))
    def _():
        term_in[...] = jnp.zeros_like(term_in)

    for m in range(2):
        right[m, :, :size] = coup_m[m].T
        right[m, :, size:] = coup_n[m].T
        for r in range(per_part):
            rows = slice(r * ROWS, (r + 1) * ROWS)
            cols = slice(m * ROWS, (m + 1) * ROWS)
            left_m[r, :, cols] = coup_m[m, :, rows]
            left_n[r, :, cols] = coup_n[m, :, rows]

    def forward(c):
        @pl.when(has_image)
        def _():
            arrived(IMG, c)

        image = held.at[IMG]
        start("near_up", both(jnp.logical_not(up_own), has_up), image, c)
        start("near_down", both(jnp.logical_not(down_own), has_down), image, c)
        start("far_up", sends["far_up"][0], image, c)
        start("far_down", sends["far_down"][0], image, c)

        @pl.when(got[A])
        def _():
            arrived(A, c)

        start("relay_up", sends["relay_up"][0], held.at[A], c)

        @pl.when(got[C])
        def _():
            arrived(C, c)

        start("relay_down", sends["relay_down"][0], held.at[C], c)

    def scale(m, i):
        return weights[0, m, i].astype(F32) / 32.0

    def term_copy(part):
        return pltpu.make_async_remote_copy(
            term_out.at[part],
            term_in.at[part],
            term_send.at[part],
            term_recv.at[part],
            device_id=(e, s - 1),
            device_id_type=MESH,
        )

    def compute(c):
        for slot in (B, D):

            @pl.when(got[slot])
            def _():
                arrived(slot, c)

        part, r = lax.div(c, per_part), lax.rem(c, per_part)
        rows = pl.ds(r * ROWS, ROWS)

        def half(m, upper, lower):
            mixed = scale(m, 0) * held[upper, part, rows].astype(F32)
            mixed += scale(m, 1) * held[lower, part, rows].astype(F32)
            return jnp.dot(
                mixed.astype(BF16), right[m], preferred_element_type=F32
            ).astype(BF16)

        both_modes = jnp.concatenate([half(0, C, A), half(1, D, B)], axis=0)
        add_term = jnp.dot(left_n[r], both_modes[:, size:], preferred_element_type=F32)

        @pl.when(r == 0)
        def _():
            term[...] = add_term

        @pl.when(r > 0)
        def _():
            term[...] += add_term

        @pl.when(r == per_part - 1)
        def _():
            term_out[part] = term[...].astype(BF16)

            @pl.when(term_goes)
            def _():
                term_copy(part).start()

        add_own = jnp.dot(left_m[r], both_modes[:, :size], preferred_element_type=F32)

        @pl.when(r == 0)
        def _():
            own[part] = add_own

        @pl.when(r > 0)
        def _():
            own[part] += add_own

    @pl.loop(0, chunks + 1)
    def _(c):
        @pl.when(c < chunks)
        def _():
            forward(c)

        @pl.when(c > 0)
        def _():
            compute(c - 1)

    for part in range(2):

        @pl.when(term_comes)
        def _():
            term_copy(part).wait_recv()

        out[0, 0, part] = (own[part] + term_in[part].astype(F32)).astype(BF16)

        @pl.when(term_goes)
        def _():
            term_copy(part).wait_send()

    @pl.loop(0, chunks)
    def _(c):
        for name, (cond, _, _) in sends.items():

            @pl.when(cond)
            def _():
                copy(name, mine, c).wait_send()


def solution(mesh):
    energies, slabs = mesh.shape["energy"], mesh.shape["slab"]

    def body(green, weights, coupling_m, coupling_n):
        size = green.shape[-1]
        per_part = size // ROWS
        vmem = pl.BlockSpec(memory_space=pltpu.VMEM)
        block = (2, size, size)
        return pl.pallas_call(
            functools.partial(kernel, energies, slabs),
            out_shape=jax.ShapeDtypeStruct(green.shape, BF16),
            in_specs=[vmem, pl.BlockSpec(memory_space=pltpu.SMEM), vmem, vmem],
            out_specs=vmem,
            scratch_shapes=[
                pltpu.VMEM((5, *block), BF16),
                pltpu.VMEM(block, F32),
                pltpu.VMEM((size, size), F32),
                pltpu.VMEM(block, BF16),
                pltpu.VMEM(block, BF16),
                pltpu.VMEM((2, size, 2 * size), BF16),
                pltpu.VMEM((per_part, size, 2 * ROWS), BF16),
                pltpu.VMEM((per_part, size, 2 * ROWS), BF16),
                pltpu.SemaphoreType.DMA((8, 2 * per_part)),
                pltpu.SemaphoreType.DMA((5, 2 * per_part)),
                pltpu.SemaphoreType.DMA((2,)),
                pltpu.SemaphoreType.DMA((2,)),
            ],
            compiler_params=pltpu.CompilerParams(collective_id=0, has_side_effects=True),
        )(green, weights, coupling_m, coupling_n)

    placed = (P("energy", "slab", None, None, None), P("energy", None, None), P(), P())
    return jax.shard_map(
        body,
        mesh=mesh,
        in_specs=placed,
        out_specs=P("energy", "slab", None, None, None),
        check_vma=False,
    )
```

```python
import functools

import jax
import jax.numpy as jnp
from jax import lax
from jax.experimental import pallas as pl
from jax.experimental.pallas import tpu as pltpu
from jax.sharding import PartitionSpec as P

MESH = pl.DeviceIdType.MESH
RUN = 16
ROWS = 128
LEAD = 2
AHEAD = 2
LATER = 2
HALF = ROWS // 2
A, B, C, D, IMG = range(5)
F32, BF16 = jnp.float32, jnp.bfloat16


def kernel(
    energies,
    slabs,
    green,
    weights,
    coup_m,
    coup_n,
    out,
    held,
    passing,
    own,
    term,
    term_out,
    term_in,
    right,
    left_m,
    left_n,
    send_sem,
    recv_sem,
    z_send,
    z_recv,
    term_send,
    term_recv,
):
    e, s = lax.axis_index("energy"), lax.axis_index("slab")
    size = green.shape[-1]
    per_part = size // ROWS
    chunks = 2 * per_part
    run, p = lax.div(e, RUN), lax.rem(e, RUN)
    first, last = run == 0, run == energies // RUN - 1

    def at(shift):
        return (run * RUN + lax.rem(p + shift + RUN, RUN), s)

    def both(*conds):
        return functools.reduce(jnp.logical_and, conds)

    def either(a, b):
        return jnp.logical_or(a, b)

    inner_up, inner_down = p >= 9, p <= 6
    has_up = both(inner_up, jnp.logical_not(first))
    has_down = both(inner_down, jnp.logical_not(last))
    has_image = either(has_up, has_down)
    got = {A: e >= 3, B: e >= 7, C: e < energies - 3, D: e < energies - 7}

    up_own, down_own = p + 3 < RUN, p >= 3
    sends = {
        "near_up": (either(up_own, has_up), at(3), A),
        "near_down": (either(down_own, has_down), at(-3), C),
        "relay_up": (both(p + 4 < RUN, got[A]), at(4), B),
        "relay_down": (both(p >= 4, got[C]), at(-4), D),
        "far_up": (both(has_up, p <= 12), at(7), B),
        "far_down": (both(has_down, p >= 3), at(-7), D),
    }
    number = {name: i for i, name in enumerate(sends)}
    term_goes, term_comes = s > 0, s < slabs - 1

    ring = 2 * slabs
    quarter = ring // 4
    runs = energies // RUN
    x, z = lax.div(run, 2), lax.rem(run, 2) * slabs + s
    step = jnp.where(inner_up, 1, -1)

    def run_of(x_there, z_there):
        return 2 * x_there + lax.div(z_there, slabs)

    def device(x_there, z_there):
        return (run_of(x_there, z_there) * RUN + p, lax.rem(z_there, slabs))

    def around(shift):
        return lax.rem(z + shift + ring, ring)

    def gives(r):
        up = both(inner_up, r < runs - 1)
        return either(up, both(inner_down, r > 0))

    ways = (quarter, -quarter)
    gives_image = gives(run)
    behind = [run_of(x, around(-w)) for w in ways]
    passes = [gives(r) for r in behind]
    pass_to = [
        device(lax.div(r + step, 2), around(w)) for r, w in zip(behind, ways)
    ]
    x_source = lax.div(run - step + 2, 2) - 1

    sources = [
        (got[A], at(-3)),
        (got[C], at(3)),
        (both(got[B], p >= 4), at(-4)),
        (both(got[B], p < 4), at(-7)),
        (both(got[D], p + 4 < RUN), at(4)),
        (both(got[D], p + 4 >= RUN), at(7)),
        (passes[0], device(x, around(-ways[0]))),
        (passes[1], device(x, around(-ways[1]))),
        (has_image, device(x_source, around(-ways[0]))),
        (has_image, device(x_source, around(-ways[1]))),
        (term_comes, (e, s + 1)),
    ]
    barrier = pltpu.get_barrier_semaphore()
    for cond, where in sources:

        @pl.when(cond)
        def _():
            pl.semaphore_signal(barrier, inc=1, device_id=where, device_id_type=MESH)

    going = [cond for cond, _, _ in sends.values()]
    going += [term_goes, gives_image, gives_image, *passes]
    pl.semaphore_wait(barrier, sum(cond.astype(jnp.int32) for cond in going))

    def piece(ref, c):
        return ref.at[lax.div(c, per_part), pl.ds(lax.rem(c, per_part) * ROWS, ROWS)]

    def copy(name, source, c):
        _, where, slot = sends[name]
        i = number[name]
        return pltpu.make_async_remote_copy(
            piece(source, c),
            piece(held.at[slot], c),
            send_sem.at[i, c],
            recv_sem.at[slot, c],
            device_id=where,
            device_id_type=MESH,
        )

    def arrived(slot, c):
        pltpu.make_async_remote_copy(
            piece(held.at[slot], c),
            piece(held.at[slot], c),
            send_sem.at[0, c],
            recv_sem.at[slot, c],
            device_id=at(3),
            device_id_type=MESH,
        ).wait_recv()

    mine = green.at[0, 0]

    def half_of(ref, c, h):
        first_row = lax.rem(c, per_part) * ROWS + h * HALF
        return ref.at[lax.div(c, per_part), pl.ds(first_row, HALF)]

    def z_copy(leg, h, c):
        source = half_of(mine, c, h) if leg == 0 else passing.at[h, c]
        target = passing.at[h, c] if leg == 0 else half_of(held.at[IMG], c, h)
        return pltpu.make_async_remote_copy(
            source,
            target,
            z_send.at[leg, h, c],
            z_recv.at[leg, h, c],
            device_id=device(x, around(ways[h])) if leg == 0 else pass_to[h],
            device_id_type=MESH,
        )

    def start(name, cond, source, c):
        @pl.when(cond)
        def _():
            copy(name, source, c).start()

    def give(c):
        @pl.when(gives_image)
        def _():
            for h in range(2):
                z_copy(0, h, c).start()

    @pl.loop(0, chunks)
    def _(c):
        @pl.when(c < AHEAD)
        def _():
            give(c)

        start("near_up", up_own, mine, c)
        start("near_down", down_own, mine, c)

    for slot, there in got.items():

        @pl.when(jnp.logical_not(there))
        def _():
            held[slot] = jnp.zeros(held.shape[1:], BF16)

    @pl.when(jnp.logical_not(term_comes))
    def _():
        term_in[...] = jnp.zeros_like(term_in)

    for m in range(2):
        right[m, :, :size] = coup_m[m].T
        right[m, :, size:] = coup_n[m].T
        for r in range(per_part):
            rows = slice(r * ROWS, (r + 1) * ROWS)
            cols = slice(m * ROWS, (m + 1) * ROWS)
            left_m[r, :, cols] = coup_m[m, :, rows]
            left_n[r, :, cols] = coup_n[m, :, rows]

    def forward(c):
        @pl.when(has_image)
        def _():
            for h in range(2):
                z_copy(1, h, c).wait_recv()

        image = held.at[IMG]
        start("near_up", both(jnp.logical_not(up_own), has_up), image, c)
        start("near_down", both(jnp.logical_not(down_own), has_down), image, c)
        start("far_up", sends["far_up"][0], image, c)
        start("far_down", sends["far_down"][0], image, c)

    def relay(c, from_up, from_down):
        for name, slot, cond in (("relay_up", A, from_up), ("relay_down", C, from_down)):

            @pl.when(both(sends[name][0], cond))
            def _():
                arrived(slot, c)
                copy(name, held.at[slot], c).start()

    def scale(m, i):
        return weights[0, m, i].astype(F32) / 32.0

    def term_copy(part):
        return pltpu.make_async_remote_copy(
            term_out.at[part],
            term_in.at[part],
            term_send.at[part],
            term_recv.at[part],
            device_id=(e, s - 1),
            device_id_type=MESH,
        )

    def compute(c):
        relayed = {A: sends["relay_up"][0], C: sends["relay_down"][0]}
        for slot, there in got.items():

            @pl.when(both(there, jnp.logical_not(relayed.get(slot, False))))
            def _():
                arrived(slot, c)

        part, r = lax.div(c, per_part), lax.rem(c, per_part)
        rows = pl.ds(r * ROWS, ROWS)

        def half(m, upper, lower):
            mixed = scale(m, 0) * held[upper, part, rows].astype(F32)
            mixed += scale(m, 1) * held[lower, part, rows].astype(F32)
            return jnp.dot(
                mixed.astype(BF16), right[m], preferred_element_type=F32
            ).astype(BF16)

        both_modes = jnp.concatenate([half(0, C, A), half(1, D, B)], axis=0)
        add_term = jnp.dot(left_n[r], both_modes[:, size:], preferred_element_type=F32)

        @pl.when(r == 0)
        def _():
            term[...] = add_term

        @pl.when(r > 0)
        def _():
            term[...] += add_term

        @pl.when(r == per_part - 1)
        def _():
            term_out[part] = term[...].astype(BF16)

            @pl.when(term_goes)
            def _():
                term_copy(part).start()

        add_own = jnp.dot(left_m[r], both_modes[:, :size], preferred_element_type=F32)

        @pl.when(r == 0)
        def _():
            own[part] = add_own

        @pl.when(r > 0)
        def _():
            own[part] += add_own

    lag = LEAD + LATER

    @pl.loop(0, chunks + lag + 1)
    def _(c):
        @pl.when(c < chunks)
        def _():
            relay(c, down_own, up_own)
            for h in range(2):

                @pl.when(passes[h])
                def _():
                    z_copy(0, h, c).wait_recv()
                    z_copy(1, h, c).start()

            @pl.when(c + AHEAD < chunks)
            def _():
                give(c + AHEAD)

        @pl.when(both(c >= LEAD, c < chunks + LEAD))
        def _():
            forward(c - LEAD)

        @pl.when(both(c >= lag, c < chunks + lag))
        def _():
            relay(c - lag, jnp.logical_not(down_own), jnp.logical_not(up_own))

        @pl.when(c > lag)
        def _():
            compute(c - lag - 1)

    for part in range(2):

        @pl.when(term_comes)
        def _():
            term_copy(part).wait_recv()

        out[0, 0, part] = (own[part] + term_in[part].astype(F32)).astype(BF16)

        @pl.when(term_goes)
        def _():
            term_copy(part).wait_send()

    @pl.loop(0, chunks)
    def _(c):
        for name, (cond, _, _) in sends.items():

            @pl.when(cond)
            def _():
                copy(name, mine, c).wait_send()

        for h in range(2):

            @pl.when(gives_image)
            def _():
                z_copy(0, h, c).wait_send()

            @pl.when(passes[h])
            def _():
                z_copy(1, h, c).wait_send()


def solution(mesh):
    energies, slabs = mesh.shape["energy"], mesh.shape["slab"]

    def body(green, weights, coupling_m, coupling_n):
        size = green.shape[-1]
        per_part = size // ROWS
        vmem = pl.BlockSpec(memory_space=pltpu.VMEM)
        block = (2, size, size)
        return pl.pallas_call(
            functools.partial(kernel, energies, slabs),
            out_shape=jax.ShapeDtypeStruct(green.shape, BF16),
            in_specs=[vmem, pl.BlockSpec(memory_space=pltpu.SMEM), vmem, vmem],
            out_specs=vmem,
            scratch_shapes=[
                pltpu.VMEM((5, *block), BF16),
                pltpu.VMEM((2, 2 * per_part, HALF, size), BF16),
                pltpu.VMEM(block, F32),
                pltpu.VMEM((size, size), F32),
                pltpu.VMEM(block, BF16),
                pltpu.VMEM(block, BF16),
                pltpu.VMEM((2, size, 2 * size), BF16),
                pltpu.VMEM((per_part, size, 2 * ROWS), BF16),
                pltpu.VMEM((per_part, size, 2 * ROWS), BF16),
                pltpu.SemaphoreType.DMA((6, 2 * per_part)),
                pltpu.SemaphoreType.DMA((4, 2 * per_part)),
                pltpu.SemaphoreType.DMA((2, 2, 2 * per_part)),
                pltpu.SemaphoreType.DMA((2, 2, 2 * per_part)),
                pltpu.SemaphoreType.DMA((2,)),
                pltpu.SemaphoreType.DMA((2,)),
            ],
            compiler_params=pltpu.CompilerParams(collective_id=0, has_side_effects=True),
        )(green, weights, coupling_m, coupling_n)

    placed = (P("energy", "slab", None, None, None), P("energy", None, None), P(), P())
    return jax.shard_map(
        body,
        mesh=mesh,
        in_specs=placed,
        out_specs=P("energy", "slab", None, None, None),
        check_vma=False,
    )
```

```python
import functools

import jax
import jax.numpy as jnp
from jax import lax
from jax.experimental import pallas as pl
from jax.experimental.pallas import tpu as pltpu
from jax.sharding import PartitionSpec as P

MESH = pl.DeviceIdType.MESH
RUN = 16
ROWS = 128
LEAD = 2
AHEAD = 2
LATER = 2
HALF = ROWS // 2
A, B, C, D, IMG = range(5)
F32, BF16 = jnp.float32, jnp.bfloat16


def kernel(
    energies,
    slabs,
    green,
    weights,
    coup_m,
    coup_n,
    out,
    held,
    passing,
    own,
    term,
    term_out,
    term_in,
    right,
    left_m,
    left_n,
    send_sem,
    recv_sem,
    z_send,
    z_recv,
    term_send,
    term_recv,
):
    e, s = lax.axis_index("energy"), lax.axis_index("slab")
    size = green.shape[-1]
    per_part = size // ROWS
    chunks = 2 * per_part
    run, p = lax.div(e, RUN), lax.rem(e, RUN)
    first, last = run == 0, run == energies // RUN - 1

    def at(shift):
        return (run * RUN + lax.rem(p + shift + RUN, RUN), s)

    def both(*conds):
        return functools.reduce(jnp.logical_and, conds)

    def either(a, b):
        return jnp.logical_or(a, b)

    inner_up, inner_down = p >= 9, p <= 6
    has_up = both(inner_up, jnp.logical_not(first))
    has_down = both(inner_down, jnp.logical_not(last))
    has_image = either(has_up, has_down)
    got = {A: e >= 3, B: e >= 7, C: e < energies - 3, D: e < energies - 7}

    up_own, down_own = p + 3 < RUN, p >= 3
    sends = {
        "near_up": (either(up_own, has_up), at(3), A),
        "near_down": (either(down_own, has_down), at(-3), C),
        "relay_up": (both(p + 4 < RUN, got[A]), at(4), B),
        "relay_down": (both(p >= 4, got[C]), at(-4), D),
        "far_up": (both(has_up, p <= 12), at(7), B),
        "far_down": (both(has_down, p >= 3), at(-7), D),
    }
    number = {name: i for i, name in enumerate(sends)}
    term_goes, term_comes = s > 0, s < slabs - 1

    ring = 2 * slabs
    quarter = ring // 4
    runs = energies // RUN
    x, z = lax.div(run, 2), lax.rem(run, 2) * slabs + s
    step = jnp.where(inner_up, 1, -1)

    def run_of(x_there, z_there):
        return 2 * x_there + lax.div(z_there, slabs)

    def device(x_there, z_there):
        return (run_of(x_there, z_there) * RUN + p, lax.rem(z_there, slabs))

    def around(shift):
        return lax.rem(z + shift + ring, ring)

    def gives(r):
        up = both(inner_up, r < runs - 1)
        return either(up, both(inner_down, r > 0))

    ways = (quarter, -quarter)
    gives_image = gives(run)
    behind = [run_of(x, around(-w)) for w in ways]
    passes = [gives(r) for r in behind]
    pass_to = [
        device(lax.div(r + step, 2), around(w)) for r, w in zip(behind, ways)
    ]
    x_source = lax.div(run - step + 2, 2) - 1

    sources = [
        (got[A], at(-3)),
        (got[C], at(3)),
        (both(got[B], p >= 4), at(-4)),
        (both(got[B], p < 4), at(-7)),
        (both(got[D], p + 4 < RUN), at(4)),
        (both(got[D], p + 4 >= RUN), at(7)),
        (passes[0], device(x, around(-ways[0]))),
        (passes[1], device(x, around(-ways[1]))),
        (has_image, device(x_source, around(-ways[0]))),
        (has_image, device(x_source, around(-ways[1]))),
        (term_comes, (e, s + 1)),
    ]
    barrier = pltpu.get_barrier_semaphore()
    for cond, where in sources:

        @pl.when(cond)
        def _():
            pl.semaphore_signal(barrier, inc=1, device_id=where, device_id_type=MESH)

    going = [cond for cond, _, _ in sends.values()]
    going += [term_goes, gives_image, gives_image, *passes]
    pl.semaphore_wait(barrier, sum(cond.astype(jnp.int32) for cond in going))

    def piece(ref, c):
        return ref.at[lax.div(c, per_part), pl.ds(lax.rem(c, per_part) * ROWS, ROWS)]

    def copy(name, source, c):
        _, where, slot = sends[name]
        i = number[name]
        return pltpu.make_async_remote_copy(
            piece(source, c),
            piece(held.at[slot], c),
            send_sem.at[i, c],
            recv_sem.at[slot, c],
            device_id=where,
            device_id_type=MESH,
        )

    def arrived(slot, c):
        pltpu.make_async_remote_copy(
            piece(held.at[slot], c),
            piece(held.at[slot], c),
            send_sem.at[0, c],
            recv_sem.at[slot, c],
            device_id=at(3),
            device_id_type=MESH,
        ).wait_recv()

    mine = green.at[0, 0]

    def half_of(ref, c, h):
        first_row = lax.rem(c, per_part) * ROWS + h * HALF
        return ref.at[lax.div(c, per_part), pl.ds(first_row, HALF)]

    def z_copy(leg, h, c):
        source = half_of(mine, c, h) if leg == 0 else passing.at[h, c]
        target = passing.at[h, c] if leg == 0 else half_of(held.at[IMG], c, h)
        return pltpu.make_async_remote_copy(
            source,
            target,
            z_send.at[leg, h, c],
            z_recv.at[leg, h, c],
            device_id=device(x, around(ways[h])) if leg == 0 else pass_to[h],
            device_id_type=MESH,
        )

    def start(name, cond, source, c):
        @pl.when(cond)
        def _():
            copy(name, source, c).start()

    def give(c):
        @pl.when(gives_image)
        def _():
            for h in range(2):
                z_copy(0, h, c).start()

    @pl.loop(0, chunks)
    def _(c):
        @pl.when(c < AHEAD)
        def _():
            give(c)

        start("near_up", up_own, mine, c)
        start("near_down", down_own, mine, c)

    for slot, there in got.items():

        @pl.when(jnp.logical_not(there))
        def _():
            held[slot] = jnp.zeros(held.shape[1:], BF16)

    @pl.when(jnp.logical_not(term_comes))
    def _():
        term_in[...] = jnp.zeros_like(term_in)

    for m in range(2):
        right[m, :, :size] = coup_m[m].T
        right[m, :, size:] = coup_n[m].T
        for r in range(per_part):
            rows = slice(r * ROWS, (r + 1) * ROWS)
            cols = slice(m * ROWS, (m + 1) * ROWS)
            left_m[r, :, cols] = coup_m[m, :, rows]
            left_n[r, :, cols] = coup_n[m, :, rows]

    def forward(c):
        @pl.when(has_image)
        def _():
            for h in range(2):
                z_copy(1, h, c).wait_recv()

        image = held.at[IMG]
        start("near_up", both(jnp.logical_not(up_own), has_up), image, c)
        start("near_down", both(jnp.logical_not(down_own), has_down), image, c)
        start("far_up", sends["far_up"][0], image, c)
        start("far_down", sends["far_down"][0], image, c)

    def relay(c, from_up, from_down):
        for name, slot, cond in (("relay_up", A, from_up), ("relay_down", C, from_down)):

            @pl.when(both(sends[name][0], cond))
            def _():
                arrived(slot, c)
                copy(name, held.at[slot], c).start()

    def scale(m, i):
        return weights[0, m, i].astype(F32) / 32.0

    def term_copy(part):
        return pltpu.make_async_remote_copy(
            term_out.at[part],
            term_in.at[part],
            term_send.at[part],
            term_recv.at[part],
            device_id=(e, s - 1),
            device_id_type=MESH,
        )

    def compute(c):
        relayed = {A: sends["relay_up"][0], C: sends["relay_down"][0]}
        for slot, there in got.items():

            @pl.when(both(there, jnp.logical_not(relayed.get(slot, False))))
            def _():
                arrived(slot, c)

        part, r = lax.div(c, per_part), lax.rem(c, per_part)
        rows = pl.ds(r * ROWS, ROWS)

        def half(m, upper, lower):
            mixed = scale(m, 0) * held[upper, part, rows].astype(F32)
            mixed += scale(m, 1) * held[lower, part, rows].astype(F32)
            return jnp.dot(
                mixed.astype(BF16), right[m], preferred_element_type=F32
            ).astype(BF16)

        both_modes = jnp.concatenate([half(0, C, A), half(1, D, B)], axis=0)
        add_term = jnp.dot(left_n[r], both_modes[:, size:], preferred_element_type=F32)

        @pl.when(r == 0)
        def _():
            term[...] = add_term

        @pl.when(r > 0)
        def _():
            term[...] += add_term

        @pl.when(r == per_part - 1)
        def _():
            term_out[part] = term[...].astype(BF16)

            @pl.when(term_goes)
            def _():
                term_copy(part).start()

        add_own = jnp.dot(left_m[r], both_modes[:, :size], preferred_element_type=F32)

        @pl.when(r == 0)
        def _():
            own[part] = add_own

        @pl.when(r > 0)
        def _():
            own[part] += add_own

    lag = LEAD + LATER

    @pl.loop(0, chunks + lag + 1)
    def _(c):
        @pl.when(c < chunks)
        def _():
            for h in range(2):

                @pl.when(passes[h])
                def _():
                    z_copy(0, h, c).wait_recv()
                    z_copy(1, h, c).start()

            @pl.when(c + AHEAD < chunks)
            def _():
                give(c + AHEAD)

        @pl.when(both(c >= LEAD, c < chunks + LEAD))
        def _():
            forward(c - LEAD)

        @pl.when(c < chunks)
        def _():
            relay(c, down_own, up_own)

        @pl.when(both(c >= lag, c < chunks + lag))
        def _():
            relay(c - lag, jnp.logical_not(down_own), jnp.logical_not(up_own))

        @pl.when(c > lag)
        def _():
            compute(c - lag - 1)

    for part in range(2):

        @pl.when(term_comes)
        def _():
            term_copy(part).wait_recv()

        out[0, 0, part] = (own[part] + term_in[part].astype(F32)).astype(BF16)

        @pl.when(term_goes)
        def _():
            term_copy(part).wait_send()

    @pl.loop(0, chunks)
    def _(c):
        for name, (cond, _, _) in sends.items():

            @pl.when(cond)
            def _():
                copy(name, mine, c).wait_send()

        for h in range(2):

            @pl.when(gives_image)
            def _():
                z_copy(0, h, c).wait_send()

            @pl.when(passes[h])
            def _():
                z_copy(1, h, c).wait_send()


def solution(mesh):
    energies, slabs = mesh.shape["energy"], mesh.shape["slab"]

    def body(green, weights, coupling_m, coupling_n):
        size = green.shape[-1]
        per_part = size // ROWS
        vmem = pl.BlockSpec(memory_space=pltpu.VMEM)
        block = (2, size, size)
        return pl.pallas_call(
            functools.partial(kernel, energies, slabs),
            out_shape=jax.ShapeDtypeStruct(green.shape, BF16),
            in_specs=[vmem, pl.BlockSpec(memory_space=pltpu.SMEM), vmem, vmem],
            out_specs=vmem,
            scratch_shapes=[
                pltpu.VMEM((5, *block), BF16),
                pltpu.VMEM((2, 2 * per_part, HALF, size), BF16),
                pltpu.VMEM(block, F32),
                pltpu.VMEM((size, size), F32),
                pltpu.VMEM(block, BF16),
                pltpu.VMEM(block, BF16),
                pltpu.VMEM((2, size, 2 * size), BF16),
                pltpu.VMEM((per_part, size, 2 * ROWS), BF16),
                pltpu.VMEM((per_part, size, 2 * ROWS), BF16),
                pltpu.SemaphoreType.DMA((6, 2 * per_part)),
                pltpu.SemaphoreType.DMA((4, 2 * per_part)),
                pltpu.SemaphoreType.DMA((2, 2, 2 * per_part)),
                pltpu.SemaphoreType.DMA((2, 2, 2 * per_part)),
                pltpu.SemaphoreType.DMA((2,)),
                pltpu.SemaphoreType.DMA((2,)),
            ],
            compiler_params=pltpu.CompilerParams(collective_id=0, has_side_effects=True),
        )(green, weights, coupling_m, coupling_n)

    placed = (P("energy", "slab", None, None, None), P("energy", None, None), P(), P())
    return jax.shard_map(
        body,
        mesh=mesh,
        in_specs=placed,
        out_specs=P("energy", "slab", None, None, None),
        check_vma=False,
    )
```
